32 devices in a mesh: space: 8 (over z, y), fsdp: 4 (over x, core).
Axes of the slice: x: 2, y: 2, z: 4, core: 2. Of those that a mesh axis runs over, the one named last changes fastest.
Arguments:
- features: bfloat16 [8, 4, 384, 384], P('space', 'fsdp'), may hold values from -60 to 60
- channel_gain: float32 [384], replicated, may hold values from 0.5 to 2
- conv_weight: bfloat16 [27, 384, 384], P(None, 'space', 'fsdp'), may hold values from -0.0625 to 0.0625
- kernel_map: int32 [8, 4, 27, 384], P('space', 'fsdp'), may hold values from 0 to 1536, as said below
- counts: int32 [8, 4, 3], P('space', 'fsdp'), may hold values from 1 to 128, as said below
- halo_list: int32 [8, 4, 1], P('space', 'fsdp'), may hold values from 0 to 2
- skip_dest: int32 [8, 4, 384, 1], P('space', 'fsdp'), may hold values from 0 to 7; in each aligned block of 384 rows (0 to 383, 384 to 767, ..., all dimensions but the last counted through in order) at most 96 rows name the same one
- out_grad: bfloat16 [8, 4, 384, 384], P('space', 'fsdp'), may hold values from -6 to 6
Outputs:
- section_out: bfloat16 [8, 4, 384, 384], P('space', 'fsdp')
- feature_grad: bfloat16 [8, 4, 384, 384], P('space', 'fsdp')
- skip_recv: bfloat16 [8, 4, 8, 96, 384], P('space', 'fsdp')
The draws below stay inside these ranges and needn't reach their ends.
Inputs may be any that keep to these rules, and one draw needn't show every extreme that they name: kernel_map[s, f, k, i] is a row of the table lookup[s, f]; the value 1536 means that offset k has no neighbour; at the middle offset every row names itself. `counts`: every device has a block with all 128 slots active. `skip_dest`: at most 96 rows of one device name one owner, and in every draw some device sends exactly 96 rows to some owner.
All inputs are finite; a program needn't handle non-finite values.
Results may differ from the reference program's by a relative error of at most 0.0045.
Values may be sent and summed in bfloat16 or wider, within the bound.
A program may use at most 64 MiB of HBM per device.

```python
import math
import jax
import jax.numpy as jnp
import numpy as np
from jax import lax

C = 384
BLK = 128
KOFF = 27
HB = 1
NB = 3
ROWS = 1536
MOST = 96
N_SPACE = 8
N_FSDP = 4


def draw_features(key, part):
    key_base, key_rows, key_cols = jax.random.split(key, 3)
    array_shape = (N_SPACE, N_FSDP, NB * BLK, C)
    row_scale = jnp.exp(jax.random.uniform(key_rows, (N_SPACE, N_FSDP, NB * BLK, 1), jnp.float32, -1.15, 1.15))
    col_scale = jnp.exp(jax.random.uniform(key_cols, (C,), jnp.float32, -1.15, 1.15))
    base_values = jax.random.truncated_normal(key_base, -5.0, 5.0, array_shape, jnp.float32)
    return (base_values * row_scale * col_scale).astype(jnp.bfloat16)


def draw_kernel_map(key, part):
    key_block, key_slot, key_gap = jax.random.split(key, 3)
    array_shape = (N_SPACE, N_FSDP, KOFF, NB * BLK)
    blocks = jax.random.randint(key_block, array_shape, 0, NB + 9 * HB)
    slot_pick = jax.random.randint(key_slot, array_shape, 0, BLK)
    absent = jax.random.randint(key_gap, array_shape, 0, 4) == 0
    picked = jnp.where(absent, ROWS, blocks * BLK + slot_pick)
    offsets = lax.broadcasted_iota(jnp.int32, array_shape, 2)
    rows_self = lax.broadcasted_iota(jnp.int32, array_shape, 3)
    return jnp.where(offsets == KOFF // 2, rows_self, picked).astype(jnp.int32)


def draw_counts(key, part):
    key_count, key_full = jax.random.split(key)
    array_shape = (N_SPACE, N_FSDP, NB)
    drawn_counts = jax.random.randint(key_count, array_shape, 1, BLK + 1)
    full_block = jax.random.randint(key_full, (N_SPACE, N_FSDP, 1), 0, NB)
    block_ids = lax.broadcasted_iota(jnp.int32, array_shape, 2)
    return jnp.where(block_ids == full_block, BLK, drawn_counts).astype(jnp.int32)


def touch_ends(entries, own_key, least, high):
    longest = entries.shape.index(max(entries.shape))
    spots = []
    for shift in (0, 1):
        where = [jax.random.randint(jax.random.fold_in(own_key, axis), (), 0, length) for axis, length in enumerate(entries.shape)]
        where[longest] = (where[longest] + shift) % entries.shape[longest]
        spots.append(tuple(where))
    return entries.at[spots[0]].set(least).at[spots[1]].set(high)


def levels(key, dims, shards, smallest, top_value):
    factor_of = 1.0
    for axis_at, shards_of in shards:
        steps = jax.random.uniform(jax.random.fold_in(jax.random.fold_in(key, 6), axis_at), (shards_of,), jnp.float32, smallest / len(shards), top_value / len(shards))
        factor_of = factor_of * jnp.repeat(jnp.exp(steps), dims[axis_at] // shards_of).reshape((-1,) + (1,) * (len(dims) - 1 - axis_at))
    return factor_of


def shared_out(key, own, number, rows, number_of, top, bound, slope):
    sequence = jax.random.permutation(key, number_of)
    crowded, ordinary = portions_of(number_of, rows * top, bound, slope, True), portions_of(number_of, rows * top, bound, slope, False)
    places = jnp.arange(number_of)

    def named(sizes, offset_by):
        used = int((sizes > 0).sum())
        fixed = max(1, used // 4)
        passed = fixed + (places - fixed + offset_by * (used - fixed)) % max(1, number_of - fixed)
        return jnp.zeros((number_of,), jnp.int32).at[sequence[jnp.where(places < fixed, places, passed)]].set(jnp.asarray(sizes, jnp.int32))

    sizes = jnp.where(number % 4 == 0, named(crowded, number // 4), named(ordinary, number - number // 4 - 1))
    mixed = jax.random.permutation(jax.random.fold_in(own, 3), number_of)
    giver, receiver = mixed[0:number_of // 2 * 2:2], mixed[1:number_of // 2 * 2:2]
    margin = jnp.minimum(sizes[giver] - 1, bound - sizes[receiver]) // 2
    margin = jnp.where((giver == sequence[0]) | (receiver == sequence[0]) | (sizes[receiver] == 0), 0, jnp.maximum(margin, 0))
    passed = jax.random.randint(jax.random.fold_in(own, 4), (number_of // 2,), 0, 1 << 20) % (margin + 1)
    sizes = sizes.at[giver].add(-passed).at[receiver].add(passed)
    items = jnp.searchsorted(jnp.cumsum(sizes), jnp.arange(rows * top), side="right").astype(jnp.int32)
    table = items.reshape(top, rows).T
    table = table[jax.random.permutation(jax.random.fold_in(own, 1), rows)]
    offset_by = jax.random.randint(jax.random.fold_in(own, 2), (rows, 1), 0, top)
    return jnp.take_along_axis(table, (jnp.arange(top)[None, :] + offset_by) % top, axis=1)


def portions_of(number_of, total, reach, lean, full):
    portions = [(1 << 20) // math.isqrt(grade ** lean) + 1 for grade in range(1, number_of + 1)]
    largest = reach if full else min(reach, max(-(-total // number_of), total * portions[0] // sum(portions)))
    least = 1 if total - largest >= number_of - 1 else 0
    holding, rest = [largest] + [least] * (number_of - 1), total - largest - least * (number_of - 1)
    while rest > 0:
        candidates = [i for i in range(1, number_of) if holding[i] < largest] or [i for i in range(1, number_of) if holding[i] < reach]
        pool, budget = sum([portions[i] for i in candidates]), rest
        for i in candidates:
            more = min(reach - holding[i], max(1, budget * portions[i] // pool), rest)
            holding[i] = holding[i] + more
            rest = rest - more
    return np.array(holding)


def scatter_about(key, shape, deviation, most, cuts=(), kind=jnp.bfloat16):
    gain = levels(key, shape, cuts, -0.22, 0.18) if cuts else 1.0
    values = jax.random.normal(key, shape, jnp.float32) * deviation * gain
    return jnp.minimum(jnp.maximum(values, -most), most).astype(kind)


def setup_inputs(seed: int = 0) -> dict:
    streams_of = jax.random.split(jax.random.key(seed), 9)
    features = draw_features(jax.random.fold_in(streams_of[8], 71), 0)
    channel_gain = jnp.clip(jnp.exp(jax.random.uniform(streams_of[1], (C,), jnp.float32, math.log(0.5), math.log(2.0))), 0.5, 2.0)
    conv_weight = scatter_about(streams_of[2], (KOFF, C, C), (KOFF * C) ** -0.5, 0.0625, ((1, 8), (2, 4)))
    kernel_map = draw_kernel_map(jax.random.fold_in(streams_of[8], 71), 0)
    counts = draw_counts(jax.random.fold_in(streams_of[8], 71), 0)
    halo_list = touch_ends(jax.random.randint(streams_of[5], (N_SPACE, N_FSDP, HB), 0, NB), jax.random.fold_in(streams_of[5], 1), 0, NB - 1).astype(jnp.int32)
    skip_dest_keys = jax.random.split(jax.random.fold_in(streams_of[6], 1), N_SPACE * N_FSDP * (NB * BLK) // (NB * BLK))
    skip_dest_turns = jax.random.permutation(jax.random.fold_in(streams_of[6], 3), N_SPACE * N_FSDP * (NB * BLK) // (NB * BLK))
    skip_dest = jax.vmap(lambda own, number: shared_out(jax.random.fold_in(streams_of[6], 2), own, number, NB * BLK, N_SPACE, 1, MOST, 2))(skip_dest_keys, skip_dest_turns).reshape((N_SPACE, N_FSDP, NB * BLK, 1))
    out_grad = scatter_about(streams_of[7], (N_SPACE, N_FSDP, NB * BLK, C), 1.0, 6.0, ((0, 8), (1, 4)))
    return {"features": features, "channel_gain": channel_gain, "conv_weight": conv_weight, "kernel_map": kernel_map, "counts": counts, "halo_list": halo_list, "skip_dest": skip_dest, "out_grad": out_grad}


NORM_EPS = 1e-06

def forward_parts(features, channel_gain, counts):
    rowcount = features.shape[2]
    slot_ids = jnp.arange(rowcount, dtype=jnp.int32)
    limits = jnp.repeat(counts, BLK, axis=2)
    active = ((slot_ids % BLK)[None, None, :] < limits).astype(jnp.float32)[..., None]
    masked = features * active.astype(jnp.bfloat16)
    masked_f = masked.astype(jnp.float32)
    rscale = lax.rsqrt(lax.optimization_barrier(jnp.mean(masked_f * masked_f, axis=-1, keepdims=True)) + NORM_EPS)
    normed = masked_f * rscale
    pre_act = normed * channel_gain
    act = jax.nn.silu(pre_act).astype(jnp.bfloat16)
    return (slot_ids, active, masked_f, rscale, normed, pre_act, act)

def reference(features, channel_gain, conv_weight, kernel_map, counts, halo_list, skip_dest, out_grad):
    space_size = N_SPACE
    fsdp_size = N_FSDP
    rowcount = NB * BLK
    slot_ids, active, masked_f, rscale, normed, pre_act, act = forward_parts(features, channel_gain, counts)
    blocked = act.reshape(space_size, fsdp_size, NB, BLK, C)
    shared = jax.vmap(jax.vmap(lambda blocks_here, chosen: blocks_here[chosen]))(blocked, halo_list)
    padded = jnp.pad(shared, ((1, 1), (1, 1), (0, 0), (0, 0), (0, 0)))
    beside_all = jnp.stack([padded[1 + shift_s:1 + shift_s + space_size, 1 + shift_f:1 + shift_f + fsdp_size] for shift_s in (-1, 0, 1) for shift_f in (-1, 0, 1)], axis=2)
    lookup = jnp.concatenate([act, beside_all.reshape(space_size, fsdp_size, 9 * HB * BLK, C), jnp.zeros((space_size, fsdp_size, 1, C), jnp.bfloat16)], axis=2)
    row_grad = out_grad * active.astype(jnp.bfloat16)

    def device_pass(packed):
        table_here, map_here, grad_here = packed

        def offset_step(state, inputs_k):
            running, table_grad = state
            weight_k, map_k = inputs_k
            running = running + jnp.dot(table_here[map_k], weight_k, preferred_element_type=jnp.float32)
            backward = jnp.dot(grad_here, weight_k.T, preferred_element_type=jnp.float32)
            table_grad = table_grad.at[map_k].add(backward)
            return ((running, table_grad), None)
        start = (jnp.zeros((rowcount, C), jnp.float32), jnp.zeros((ROWS + 1, C), jnp.float32))
        (running, table_grad), _ = lax.scan(offset_step, start, (conv_weight, map_here))
        return (running, table_grad[:ROWS])
    conv_sum, lookup_grad = lax.map(device_pass, (lookup.reshape(space_size * fsdp_size, ROWS + 1, C), kernel_map.reshape(space_size * fsdp_size, KOFF, rowcount), row_grad.reshape(space_size * fsdp_size, rowcount, C)))
    conv_sum = conv_sum.reshape(space_size, fsdp_size, rowcount, C)
    section_out = ((masked_f + conv_sum) * active).astype(jnp.bfloat16)
    owners = skip_dest[..., 0]
    earlier = (owners[..., None, :] == owners[..., :, None]) & (slot_ids[None, :] < slot_ids[:, None])
    placing = lax.optimization_barrier(jnp.sum(earlier.astype(jnp.int32), axis=-1))
    target = owners * MOST + placing

    def place_rows(rows_here, target_here):
        return jnp.zeros((space_size * MOST, C), jnp.bfloat16).at[target_here].set(rows_here)
    outbox = jax.vmap(jax.vmap(place_rows))(section_out, target)
    skip_recv = jnp.transpose(outbox.reshape(space_size, fsdp_size, space_size, MOST, C), (2, 1, 0, 3, 4))
    lookup_grad = lookup_grad.reshape(space_size, fsdp_size, ROWS, C)
    halo_grad = lookup_grad[:, :, rowcount:].reshape(space_size, fsdp_size, 3, 3, HB, BLK, C)
    halo_pad = jnp.pad(halo_grad, ((1, 1), (1, 1), (0, 0), (0, 0), (0, 0), (0, 0), (0, 0)))
    returned = jnp.zeros((space_size, fsdp_size, HB, BLK, C), jnp.float32)
    for shift_s in (-1, 0, 1):
        for shift_f in (-1, 0, 1):
            returned = returned + halo_pad[1 + shift_s:1 + shift_s + space_size, 1 + shift_f:1 + shift_f + fsdp_size, 1 - shift_s, 1 - shift_f]
    own_grad = lookup_grad[:, :, :rowcount].reshape(space_size, fsdp_size, NB, BLK, C)
    act_grad = jax.vmap(jax.vmap(lambda grad_here, chosen, extra: grad_here.at[chosen].add(extra)))(own_grad, halo_list, returned)
    act_grad = act_grad.reshape(space_size, fsdp_size, rowcount, C)
    sigmoid_pre = jax.nn.sigmoid(pre_act)
    pre_grad = act_grad * sigmoid_pre * (1.0 + pre_act * (1.0 - sigmoid_pre))
    normed_grad = pre_grad * channel_gain
    masked_grad = rscale * (normed_grad - normed * lax.optimization_barrier(jnp.mean(normed_grad * normed, axis=-1, keepdims=True)))
    feature_grad = ((row_grad.astype(jnp.float32) + masked_grad) * active).astype(jnp.bfloat16)
    return (section_out, feature_grad, skip_recv)
```

```python
import functools

import jax
import jax.numpy as jnp
from jax import lax
from jax.experimental import pallas as pl
from jax.experimental.pallas import tpu as pltpu
from jax.sharding import PartitionSpec as P

BLK = 128
KOFF = 27
HB = 1
NB = 3
ROWS = 1536


NORM_EPS = 1e-06


def padded(cells, sides, width):
    for axis, dim in sides:
        count = lax.axis_size(axis)
        ends = count - 1
        head = lax.slice_in_dim(cells, 0, width, axis=dim)
        tail = lax.slice_in_dim(cells, cells.shape[dim] - width, cells.shape[dim], axis=dim)
        cells = jnp.concatenate(
            [
                lax.ppermute(tail, axis, [(i, (i + 1) % count) for i in range(ends)]),
                cells,
                lax.ppermute(head, axis, [((i + 1) % count, i) for i in range(ends)]),
            ],
            axis=dim,
        )
    return cells


def passed_along(x, axis, by):
    count = lax.axis_size(axis)
    pairs = [(i, i + by) for i in range(count) if 0 <= i + by < count]
    return lax.ppermute(x, axis, pairs)


def shards_plain(features, channel_gain, conv_weight, kernel_map, counts, halo_list, skip_dest, out_grad):
    own_rows = features[0, 0]
    rowcount = own_rows.shape[0]
    width = own_rows.shape[1]
    slot_ids = jnp.arange(rowcount, dtype=jnp.int32)
    limits = jnp.repeat(counts[0, 0], BLK)
    active = (slot_ids % BLK < limits).astype(jnp.float32)[:, None]
    masked = own_rows * active.astype(jnp.bfloat16)
    masked_f = masked.astype(jnp.float32)
    rscale = lax.rsqrt(jnp.mean(masked_f * masked_f, axis=-1, keepdims=True) + NORM_EPS)
    normed = masked_f * rscale
    pre_act = normed * channel_gain
    act = jax.nn.silu(pre_act).astype(jnp.bfloat16)
    shared = act.reshape(NB, BLK, width)[halo_list[0, 0]]
    beside_all = padded(shared[None, None], (("space", 0), ("fsdp", 1)), 1)
    lookup = jnp.concatenate(
        [act, beside_all.reshape(9 * HB * BLK, width), jnp.zeros((1, width), jnp.bfloat16)], axis=0
    )
    row_grad = out_grad[0, 0] * active.astype(jnp.bfloat16)
    groups = KOFF // 3
    weight_groups = conv_weight.reshape(groups, 3, conv_weight.shape[1], conv_weight.shape[2])
    map_groups = kernel_map[0, 0].reshape(groups, 3, rowcount)

    def group_step(state, inputs_g):
        running, table_grad = state
        weight_piece, neighbours = inputs_g
        widened = lax.all_gather(weight_piece, "fsdp", axis=2, tiled=True)
        full_weights = lax.all_gather(widened, "space", axis=1, tiled=True)
        picked = lookup[neighbours]
        running = running + jnp.einsum(
            "kvc,kcd->vd", picked, full_weights, preferred_element_type=jnp.float32
        )
        backward = jnp.einsum(
            "vd,kcd->kvc", row_grad, full_weights, preferred_element_type=jnp.float32
        )
        table_grad = table_grad.at[neighbours.reshape(-1)].add(backward.reshape(-1, width))
        return ((running, table_grad), None)

    start = (jnp.zeros((rowcount, width), jnp.float32), jnp.zeros((ROWS + 1, width), jnp.float32))
    (conv_sum, table_grad), _ = lax.scan(group_step, start, (weight_groups, map_groups))
    section_out = ((masked_f + conv_sum) * active).astype(jnp.bfloat16)
    owners = skip_dest[0, 0, :, 0]
    earlier = (owners[None, :] == owners[:, None]) & (slot_ids[None, :] < slot_ids[:, None])
    placing = jnp.sum(earlier.astype(jnp.int32), axis=1)
    space_size = lax.axis_size("space")
    capacity = max(2, 2 * rowcount // space_size)
    outbox = (
        jnp.zeros((space_size * capacity, width), jnp.bfloat16)
        .at[owners * capacity + placing]
        .set(section_out)
    )
    received = lax.all_to_all(
        outbox.reshape(space_size, capacity, width),
        "space",
        split_axis=0,
        concat_axis=0,
        tiled=True,
    )
    halo_grad = table_grad[rowcount : rowcount + 9 * HB * BLK].reshape(3, 3, HB, BLK, width)
    middle = halo_grad[1]
    for direction in (1, -1):
        middle = middle + passed_along(
            halo_grad[1 + direction].astype(jnp.bfloat16), "space", direction
        ).astype(jnp.float32)
    returned = middle[1]
    for direction in (1, -1):
        returned = returned + passed_along(
            middle[1 + direction].astype(jnp.bfloat16), "fsdp", direction
        ).astype(jnp.float32)
    act_grad = table_grad[:rowcount].reshape(NB, BLK, width).at[halo_list[0, 0]].add(returned)
    act_grad = act_grad.reshape(rowcount, width)
    sigmoid_pre = jax.nn.sigmoid(pre_act)
    pre_grad = act_grad * sigmoid_pre * (1.0 + pre_act * (1.0 - sigmoid_pre))
    normed_grad = pre_grad * channel_gain
    masked_grad = rscale * (
        normed_grad - normed * jnp.mean(normed_grad * normed, axis=-1, keepdims=True)
    )
    feature_grad = ((row_grad.astype(jnp.float32) + masked_grad) * active).astype(jnp.bfloat16)
    return (section_out[None, None], feature_grad[None, None], received[None, None])


LANES = 128
Q = 3
MESH = pl.DeviceIdType.MESH
F32 = jnp.float32
BF16 = jnp.bfloat16


def moved(x, shift):
    shift = shift % LANES
    return x if shift == 0 else pltpu.roll(x, shift, 1)


def regroup(x, from_of, to_of, width, pieces):
    lanes = lax.broadcasted_iota(jnp.int32, (x.shape[0], LANES), 1)
    tiles = {}
    for p in range(pieces):
        r = 0
        while r < width:
            src, dst = from_of(p, r), to_of(p, r)
            span = min(width - r, LANES - src % LANES, LANES - dst % LANES)
            at = src // LANES * LANES
            value = moved(x[:, at : at + LANES], dst - src)
            low = dst % LANES
            held = tiles.get(dst // LANES, jnp.zeros_like(value))
            tiles[dst // LANES] = jnp.where((lanes >= low) & (lanes < low + span), value, held)
            r += span
    return jnp.concatenate([tiles[t] for t in range(len(tiles))], axis=1)


def norm_parts(feat, active, gain):
    masked = feat.astype(F32) * active
    rscale = lax.rsqrt(jnp.mean(masked * masked, axis=-1, keepdims=True) + NORM_EPS)
    normed = masked * rscale
    return masked, rscale, normed, normed * gain


def section_kernel(
    dims, h_ref, feat, gain, active, og, wire, nmap, tgt,
    sec, fgrad, recv,
    wbuf, lookup, pb, conv, shared, rgp, w3, gsend, grecv, outbox,
    wsend, wrecv, hsend, hrecv, ssend, srecv, bsend, brecv, own_sem,
):
    S, F, Z, G, K4 = dims
    Y = 2
    rows, C = feat.shape
    width = C // F
    table = lookup.shape[0]
    s = lax.axis_index("space")
    f = lax.axis_index("fsdp")
    z, y = s // Y, s % Y
    fx = (f + 2) % F
    fp = f + 1 - 2 * (f % 2)
    sy = s + 1 - 2 * y

    def remote(src, dst, a, b, ss, ff):
        return pltpu.make_async_remote_copy(
            src_ref=src, dst_ref=dst, send_sem=a, recv_sem=b, device_id=(ss, ff), device_id_type=MESH
        )

    def inside(ds, df):
        return (s + ds >= 0) & (s + ds < S) & (f + df >= 0) & (f + df < F)

    around = [(ds, df) for ds in (-1, 0, 1) for df in (-1, 0, 1)]

    own = pltpu.make_async_copy(wire, wbuf.at[:, f, :, z, y], own_sem)
    own.start()
    masked, rscale, normed, pre = norm_parts(feat[...], active[...], gain[...])
    act = (pre / (1.0 + jnp.exp(-pre))).astype(BF16)
    lookup[0:rows, :] = act
    h = h_ref[0]
    share = act[0:BLK]
    for b in range(1, NB):
        share = jnp.where(h == b, act[b * BLK : (b + 1) * BLK].astype(F32), share.astype(F32)).astype(BF16)
    shared[...] = share
    for n, (ds, df) in enumerate(around):
        if ds == 0 and df == 0:
            lookup[rows + n * BLK : rows + (n + 1) * BLK, :] = share
        else:

            @pl.when(jnp.logical_not(inside(ds, df)))
            def _():
                lookup[rows + n * BLK : rows + (n + 1) * BLK, :] = jnp.zeros((BLK, C), BF16)

            @pl.when(jnp.logical_not(inside(-ds, -df)))
            def _():
                grecv[n] = jnp.zeros((BLK, C), BF16)

    rg = (og[...].astype(F32) * active[...])
    rgp[...] = regroup(
        rg, lambda p, r: p * width + r, lambda p, r: p * LANES + r, width, F
    ).astype(BF16)
    conv[...] = jnp.zeros_like(conv)

    barrier = pltpu.get_barrier_semaphore()
    for d in range(1, S):
        pl.semaphore_signal(barrier, inc=1, device_id=((s + d) % S, f), device_id_type=MESH)
    for d in range(1, F):
        pl.semaphore_signal(barrier, inc=1, device_id=(s, (f + d) % F), device_id_type=MESH)
    for ds, df in around:
        if ds and df:
            pl.semaphore_signal(
                barrier, inc=1, device_id=((s + ds + S) % S, (f + df + F) % F), device_id_type=MESH
            )
    pl.semaphore_wait(barrier, S + F - 2 + 4)

    def halo(n, ds, df):
        return remote(
            shared, lookup.at[pl.ds(rows + n * BLK, BLK)], hsend.at[n], hrecv.at[n], s - ds, f - df
        )

    def first(g, d):
        return remote(
            wire.at[g], wbuf.at[g, f, :, z, y], wsend.at[g, d - 1], wrecv.at[g, d - 1],
            ((z + d) % Z) * Y + y, f,
        )

    def strip(g, col, i, ss, ff):
        ref = wbuf.at[g, col, :, :, y]
        return remote(ref, ref, wsend.at[g, i], wrecv.at[g, i], ss, ff)

    def column(g, col, i, ss, ff):
        ref = wbuf.at[g, col]
        return remote(ref, ref, wsend.at[g, i], wrecv.at[g, i], ss, ff)

    B0 = Z - 1

    def second_a(g):
        return strip(g, f, B0, sy, f)

    def second_b(g):
        return strip(g, f, B0, s, fx)

    def third_a(g):
        return [column(g, f, B0 + 1, s, fx), column(g, f, B0 + 2, s, fp)]

    def third_b(g):
        return [strip(g, f, B0 + 1, sy, f), strip(g, fx, B0 + 4, sy, f)]

    def fourth_a(g):
        return [column(g, fx, B0 + 3, s, fp)]

    def fourth_b(g):
        return [column(g, f, B0 + 2, s, fp), column(g, fx, B0 + 3, s, fp)]

    for n, (ds, df) in enumerate(around):
        if ds or df:

            @pl.when(inside(-ds, -df))
            def _():
                halo(n, ds, df).start()

    @pl.loop(0, G)
    def _(g):
        for d in range(1, Z):
            first(g, d).start()

    own.wait()
    for n, (ds, df) in enumerate(around):
        if ds or df:

            @pl.when(inside(ds, df))
            def _():
                halo(n, ds, df).wait_recv()

    lane_u = lax.broadcasted_iota(jnp.int32, (rows, table), 1)

    def gather(k):
        line = jnp.broadcast_to(nmap[k], (8, rows))
        ids = jnp.transpose(line)[:, 0:1]
        pick = jnp.where(lane_u == ids, 1.0, 0.0).astype(BF16)
        pb[k] = jnp.dot(pick, lookup[...], preferred_element_type=F32).astype(BF16)

    def whole(g, j):
        return jnp.concatenate([wbuf[g, p, j].reshape(C, LANES) for p in range(F)], axis=1)

    def use(g, j, weights):
        k = g * K4 + j
        conv[...] += jnp.dot(pb[k], weights, preferred_element_type=F32)
        pb[k] = lax.dot_general(
            rgp[...], weights, (((1,), (1,)), ((), ())), preferred_element_type=F32
        ).astype(BF16)

    @pl.loop(0, G + 3)
    def _(t):
        @pl.when(t < G)
        def _():
            for d in range(1, Z):
                first(t, d).wait_recv()

            @pl.when(t % 2 == 0)
            def _():
                second_a(t).start()

            @pl.when(t % 2 == 1)
            def _():
                second_b(t).start()

        g3 = t - 1

        @pl.when((g3 >= 0) & (g3 < G))
        def _():
            @pl.when(g3 % 2 == 0)
            def _():
                second_a(g3).wait_recv()
                for c in third_a(g3):
                    c.start()

            @pl.when(g3 % 2 == 1)
            def _():
                second_b(g3).wait_recv()
                for c in third_b(g3):
                    c.start()

        g4 = t - 2

        @pl.when((g4 >= 0) & (g4 < G))
        def _():
            @pl.when(g4 % 2 == 0)
            def _():
                third_a(g4)[0].wait_recv()
                for c in fourth_a(g4):
                    c.start()

            @pl.when(g4 % 2 == 1)
            def _():
                for c in third_b(g4):
                    c.wait_recv()
                for c in fourth_b(g4):
                    c.start()

        @pl.when(t < G)
        def _():
            @pl.loop(0, K4)
            def _(j):
                gather(t * K4 + j)

        g5 = t - 3

        @pl.when(g5 >= 0)
        def _():
            for c in fourth_b(g5):
                c.wait_recv()
            lanes = lax.broadcasted_iota(jnp.int32, (C, LANES), 1)
            piece = LANES - width
            for p in range(F):
                tile = jnp.zeros((C, LANES), F32)
                for q in range(Q):
                    part = moved(wbuf[g5, p, q].reshape(C, LANES).astype(F32), q * piece - width)
                    tile = jnp.where((lanes >= q * piece) & (lanes < (q + 1) * piece), part, tile)
                w3[:, p * LANES : (p + 1) * LANES] = tile.astype(BF16)

            @pl.loop(0, Q)
            def _(j):
                use(g5, j, whole(g5, j))

            use(g5, Q, w3[...])

    total = regroup(conv[...], lambda p, r: p * LANES + r, lambda p, r: p * width + r, width, F)
    out = ((feat[...].astype(F32) * active[...] + total) * active[...]).astype(BF16)
    sec[...] = out
    cap = recv.shape[1]
    slots = lax.broadcasted_iota(jnp.int32, (S * cap, rows), 0)
    place = jnp.where(slots == tgt[...], 1.0, 0.0).astype(BF16)
    outbox[...] = jnp.dot(place, out, preferred_element_type=F32).astype(BF16).reshape(S, cap, C)

    def skip(d):
        o = (s + d) % S
        return remote(outbox.at[o], recv.at[s], ssend.at[d - 1], srecv.at[d - 1], o, f)

    def scatter(u0):
        def step(g, acc):
            base = lax.broadcasted_iota(jnp.int32, (rows, rows), 0) + u0
            hot = jnp.concatenate(
                [jnp.where(base == nmap[g * K4 + j], 1.0, 0.0).astype(BF16) for j in range(K4)], axis=1
            )
            return acc + jnp.dot(
                hot, pb[pl.ds(g * K4, K4)].reshape(K4 * rows, C), preferred_element_type=F32
            )

        return step

    def grad(n, ds, df):
        return remote(gsend.at[n], grecv.at[n], bsend.at[n], brecv.at[n], s + ds, f + df)

    per = rows // BLK

    def send_grads(c):
        for n in range(c * per, (c + 1) * per):
            ds, df = around[n]
            if ds or df:

                @pl.when(inside(ds, df))
                def _():
                    grad(n, ds, df).start()

    keep = pltpu.make_async_copy(outbox.at[s], recv.at[s], own_sem)

    @pl.loop(0, len(around) // per)
    def _(c):
        conv[:, 0:C] = jnp.zeros((rows, C), F32)

        @pl.loop(0, G)
        def _(g):
            conv[:, 0:C] = scatter((c + 1) * rows)(g, conv[:, 0:C])

        gsend[pl.ds(c * per, per)] = conv[:, 0:C].astype(BF16).reshape(per, BLK, C)

        @pl.when(c == 0)
        def _():
            for d in range(1, S):
                skip(d).start()
            keep.start()

        for cc in range(1, len(around) // per):

            @pl.when(c == cc)
            def _():
                send_grads(cc - 1)

        @pl.when(c == (len(around) // per) // 2)
        def _():
            lo = (len(around) // 2 % per) * BLK
            grecv[len(around) // 2] = conv[lo : lo + BLK, 0:C].astype(BF16)

    conv[:, 0:C] = scatter(0)(0, jnp.zeros((rows, C), F32))
    send_grads(len(around) // per - 1)

    @pl.loop(1, G)
    def _(g):
        conv[:, 0:C] = scatter(0)(g, conv[:, 0:C])

    for n, (ds, df) in enumerate(around):
        if ds or df:

            @pl.when(inside(-ds, -df))
            def _():
                grad(n, ds, df).wait_recv()

    back = jnp.zeros((BLK, C), F32)
    for n in range(len(around)):
        back = back + grecv[n].astype(F32)
    for b in range(NB):
        r0 = b * BLK
        act_b = active[r0 : r0 + BLK]
        masked, rscale, normed, pre = norm_parts(feat[r0 : r0 + BLK], act_b, gain[...])
        ag = conv[r0 : r0 + BLK, 0:C] + jnp.where(h == b, back, 0.0)
        sig = 1.0 / (1.0 + jnp.exp(-pre))
        ng = ag * sig * (1.0 + pre * (1.0 - sig)) * gain[...]
        mg = rscale * (ng - normed * jnp.mean(ng * normed, axis=-1, keepdims=True))
        fgrad[r0 : r0 + BLK] = (
            (og[r0 : r0 + BLK].astype(F32) * act_b + mg) * act_b
        ).astype(BF16)

    keep.wait()
    for d in range(1, S):
        skip(d).wait()
    for n, (ds, df) in enumerate(around):
        if ds or df:

            @pl.when(inside(-ds, -df))
            def _():
                halo(n, ds, df).wait_send()

            @pl.when(inside(ds, df))
            def _():
                grad(n, ds, df).wait_send()

    @pl.loop(0, G)
    def _(g):
        for d in range(1, Z):
            first(g, d).wait_send()

        @pl.when(g % 2 == 0)
        def _():
            for c in [second_a(g)] + third_a(g) + fourth_a(g):
                c.wait_send()

        @pl.when(g % 2 == 1)
        def _():
            for c in [second_b(g)] + third_b(g) + fourth_b(g):
                c.wait_send()


def shards(mesh, features, channel_gain, conv_weight, kernel_map, counts, halo_list, skip_dest, out_grad):
    S, F = mesh.shape["space"], mesh.shape["fsdp"]
    koff, cin, width = conv_weight.shape
    rows, C = features.shape[2:]
    piece = LANES - width
    fits = F == 4 and S % 2 == 0 and cin % 16 == 0 and width == Q * piece and halo_list.shape[2] == 1
    if not (fits and rows == NB * BLK and 9 % NB == 0 and C == F * width):
        return shards_plain(
            features, channel_gain, conv_weight, kernel_map, counts, halo_list, skip_dest, out_grad
        )
    Z, K4 = S // 2, Q + 1
    G = -(-koff // K4)
    slot_ids = jnp.arange(rows, dtype=jnp.int32)
    active = (slot_ids % BLK < jnp.repeat(counts[0, 0], BLK)).astype(F32)[:, None]
    w = jnp.pad(conv_weight, ((0, G * K4 - koff), (0, 0), (0, 0))).reshape(G, K4, cin, width)
    extra = w[:, Q].reshape(G, cin, Q, piece).transpose(0, 2, 1, 3)
    wire = jnp.concatenate([w[:, :Q], extra], axis=-1)
    table = rows + 9 * BLK
    nmap = jnp.pad(kernel_map[0, 0], ((0, G * K4 - koff), (0, 0)), constant_values=table)[:, None, :]
    owners = skip_dest[0, 0, :, 0]
    earlier = (owners[None, :] == owners[:, None]) & (slot_ids[None, :] < slot_ids[:, None])
    placing = jnp.sum(earlier.astype(jnp.int32), axis=1)
    cap = max(2, 2 * rows // S)
    tgt = (owners * cap + placing)[None, :]
    vm = pl.BlockSpec(memory_space=pltpu.VMEM)
    dma = pltpu.SemaphoreType.DMA
    sec, fgrad, recv = pl.pallas_call(
        functools.partial(section_kernel, (S, F, Z, G, K4)),
        out_shape=(
            jax.ShapeDtypeStruct((rows, C), BF16),
            jax.ShapeDtypeStruct((rows, C), BF16),
            jax.ShapeDtypeStruct((S, cap, C), BF16),
        ),
        in_specs=[pl.BlockSpec(memory_space=pltpu.SMEM)] + [vm] * 7,
        out_specs=(vm, vm, vm),
        scratch_shapes=[
            pltpu.VMEM((G, F, Q, Z, 2, cin, LANES), BF16),
            pltpu.VMEM((table, C), BF16),
            pltpu.VMEM((G * K4, rows, C), BF16),
            pltpu.VMEM((rows, F * LANES), F32),
            pltpu.VMEM((BLK, C), BF16),
            pltpu.VMEM((rows, F * LANES), BF16),
            pltpu.VMEM((C, F * LANES), BF16),
            pltpu.VMEM((9, BLK, C), BF16),
            pltpu.VMEM((9, BLK, C), BF16),
            pltpu.VMEM((S, cap, C), BF16),
            dma((G, Z + 4)),
            dma((G, Z + 4)),
            dma((9,)),
            dma((9,)),
            dma((S - 1,)),
            dma((S - 1,)),
            dma((9,)),
            dma((9,)),
            dma,
        ],
        compiler_params=pltpu.CompilerParams(collective_id=0, has_side_effects=True),
        name="section",
    )(halo_list[0, 0], features[0, 0], channel_gain[None, :], active, out_grad[0, 0], wire, nmap, tgt)
    return (sec[None, None], fgrad[None, None], recv[None, None])


def solution(mesh):
    return jax.shard_map(
        functools.partial(shards, mesh),
        mesh=mesh,
        in_specs=(
            P("space", "fsdp", None, None),
            P(),
            P(None, "space", "fsdp"),
            P("space", "fsdp", None, None),
            P("space", "fsdp", None),
            P("space", "fsdp", None),
            P("space", "fsdp", None, None),
            P("space", "fsdp", None, None),
        ),
        out_specs=(
            P("space", "fsdp", None, None),
            P("space", "fsdp", None, None),
            P("space", "fsdp", None, None, None),
        ),
        check_vma=False,
    )
```

```python
import functools

import jax
import jax.numpy as jnp
from jax import lax
from jax.experimental import pallas as pl
from jax.experimental.pallas import tpu as pltpu
from jax.sharding import PartitionSpec as P

BLK = 128
KOFF = 27
HB = 1
NB = 3
ROWS = 1536


NORM_EPS = 1e-06


def padded(cells, sides, width):
    for axis, dim in sides:
        count = lax.axis_size(axis)
        ends = count - 1
        head = lax.slice_in_dim(cells, 0, width, axis=dim)
        tail = lax.slice_in_dim(cells, cells.shape[dim] - width, cells.shape[dim], axis=dim)
        cells = jnp.concatenate(
            [
                lax.ppermute(tail, axis, [(i, (i + 1) % count) for i in range(ends)]),
                cells,
                lax.ppermute(head, axis, [((i + 1) % count, i) for i in range(ends)]),
            ],
            axis=dim,
        )
    return cells


def passed_along(x, axis, by):
    count = lax.axis_size(axis)
    pairs = [(i, i + by) for i in range(count) if 0 <= i + by < count]
    return lax.ppermute(x, axis, pairs)


def shards_plain(features, channel_gain, conv_weight, kernel_map, counts, halo_list, skip_dest, out_grad):
    own_rows = features[0, 0]
    rowcount = own_rows.shape[0]
    width = own_rows.shape[1]
    slot_ids = jnp.arange(rowcount, dtype=jnp.int32)
    limits = jnp.repeat(counts[0, 0], BLK)
    active = (slot_ids % BLK < limits).astype(jnp.float32)[:, None]
    masked = own_rows * active.astype(jnp.bfloat16)
    masked_f = masked.astype(jnp.float32)
    rscale = lax.rsqrt(jnp.mean(masked_f * masked_f, axis=-1, keepdims=True) + NORM_EPS)
    normed = masked_f * rscale
    pre_act = normed * channel_gain
    act = jax.nn.silu(pre_act).astype(jnp.bfloat16)
    shared = act.reshape(NB, BLK, width)[halo_list[0, 0]]
    beside_all = padded(shared[None, None], (("space", 0), ("fsdp", 1)), 1)
    lookup = jnp.concatenate(
        [act, beside_all.reshape(9 * HB * BLK, width), jnp.zeros((1, width), jnp.bfloat16)], axis=0
    )
    row_grad = out_grad[0, 0] * active.astype(jnp.bfloat16)
    groups = KOFF // 3
    weight_groups = conv_weight.reshape(groups, 3, conv_weight.shape[1], conv_weight.shape[2])
    map_groups = kernel_map[0, 0].reshape(groups, 3, rowcount)

    def group_step(state, inputs_g):
        running, table_grad = state
        weight_piece, neighbours = inputs_g
        widened = lax.all_gather(weight_piece, "fsdp", axis=2, tiled=True)
        full_weights = lax.all_gather(widened, "space", axis=1, tiled=True)
        picked = lookup[neighbours]
        running = running + jnp.einsum(
            "kvc,kcd->vd", picked, full_weights, preferred_element_type=jnp.float32
        )
        backward = jnp.einsum(
            "vd,kcd->kvc", row_grad, full_weights, preferred_element_type=jnp.float32
        )
        table_grad = table_grad.at[neighbours.reshape(-1)].add(backward.reshape(-1, width))
        return ((running, table_grad), None)

    start = (jnp.zeros((rowcount, width), jnp.float32), jnp.zeros((ROWS + 1, width), jnp.float32))
    (conv_sum, table_grad), _ = lax.scan(group_step, start, (weight_groups, map_groups))
    section_out = ((masked_f + conv_sum) * active).astype(jnp.bfloat16)
    owners = skip_dest[0, 0, :, 0]
    earlier = (owners[None, :] == owners[:, None]) & (slot_ids[None, :] < slot_ids[:, None])
    placing = jnp.sum(earlier.astype(jnp.int32), axis=1)
    space_size = lax.axis_size("space")
    capacity = max(2, 2 * rowcount // space_size)
    outbox = (
        jnp.zeros((space_size * capacity, width), jnp.bfloat16)
        .at[owners * capacity + placing]
        .set(section_out)
    )
    received = lax.all_to_all(
        outbox.reshape(space_size, capacity, width),
        "space",
        split_axis=0,
        concat_axis=0,
        tiled=True,
    )
    halo_grad = table_grad[rowcount : rowcount + 9 * HB * BLK].reshape(3, 3, HB, BLK, width)
    middle = halo_grad[1]
    for direction in (1, -1):
        middle = middle + passed_along(
            halo_grad[1 + direction].astype(jnp.bfloat16), "space", direction
        ).astype(jnp.float32)
    returned = middle[1]
    for direction in (1, -1):
        returned = returned + passed_along(
            middle[1 + direction].astype(jnp.bfloat16), "fsdp", direction
        ).astype(jnp.float32)
    act_grad = table_grad[:rowcount].reshape(NB, BLK, width).at[halo_list[0, 0]].add(returned)
    act_grad = act_grad.reshape(rowcount, width)
    sigmoid_pre = jax.nn.sigmoid(pre_act)
    pre_grad = act_grad * sigmoid_pre * (1.0 + pre_act * (1.0 - sigmoid_pre))
    normed_grad = pre_grad * channel_gain
    masked_grad = rscale * (
        normed_grad - normed * jnp.mean(normed_grad * normed, axis=-1, keepdims=True)
    )
    feature_grad = ((row_grad.astype(jnp.float32) + masked_grad) * active).astype(jnp.bfloat16)
    return (section_out[None, None], feature_grad[None, None], received[None, None])


LANES = 128
Q = 3
MESH = pl.DeviceIdType.MESH
F32 = jnp.float32
BF16 = jnp.bfloat16


def moved(x, shift):
    shift = shift % LANES
    return x if shift == 0 else pltpu.roll(x, shift, 1)


def regroup(x, from_of, to_of, width, pieces):
    lanes = lax.broadcasted_iota(jnp.int32, (x.shape[0], LANES), 1)
    tiles = {}
    for p in range(pieces):
        r = 0
        while r < width:
            src, dst = from_of(p, r), to_of(p, r)
            span = min(width - r, LANES - src % LANES, LANES - dst % LANES)
            at = src // LANES * LANES
            value = moved(x[:, at : at + LANES], dst - src)
            low = dst % LANES
            held = tiles.get(dst // LANES, jnp.zeros_like(value))
            tiles[dst // LANES] = jnp.where((lanes >= low) & (lanes < low + span), value, held)
            r += span
    return jnp.concatenate([tiles[t] for t in range(len(tiles))], axis=1)


def norm_parts(feat, active, gain):
    masked = feat.astype(F32) * active
    rscale = lax.rsqrt(jnp.mean(masked * masked, axis=-1, keepdims=True) + NORM_EPS)
    normed = masked * rscale
    return masked, rscale, normed, normed * gain


def section_kernel(
    dims, h_ref, counts, feat, gain, og, wire, maps, owners,
    sec, fgrad, recv,
    active, nmap, tgt, wbuf, lookup, pb, conv, shared, rgp, w3, gsend, grecv, outbox,
    wsend, wrecv, hsend, hrecv, ssend, srecv, bsend, brecv, own_sem,
):
    S, F, Z, G, K4 = dims
    Y = 2
    rows, C = feat.shape
    width = C // F
    table = lookup.shape[0]
    s = lax.axis_index("space")
    f = lax.axis_index("fsdp")
    z, y = s // Y, s % Y
    fx = (f + 2) % F
    fp = f + 1 - 2 * (f % 2)
    sy = s + 1 - 2 * y

    def remote(src, dst, a, b, ss, ff):
        return pltpu.make_async_remote_copy(
            src_ref=src, dst_ref=dst, send_sem=a, recv_sem=b, device_id=(ss, ff), device_id_type=MESH
        )

    def inside(ds, df):
        return (s + ds >= 0) & (s + ds < S) & (f + df >= 0) & (f + df < F)

    around = [(ds, df) for ds in (-1, 0, 1) for df in (-1, 0, 1)]

    own = pltpu.make_async_copy(wire, wbuf.at[:, f, :, z, y], own_sem)
    own.start()
    slot = lax.broadcasted_iota(jnp.int32, (BLK, 1), 0)
    for b in range(NB):
        active[b * BLK : (b + 1) * BLK] = jnp.where(slot < counts[b], 1.0, 0.0)
    gains = gain[...].reshape(1, C)
    koff = maps.shape[0]
    nmap[0:koff] = maps[...]
    nmap[koff:] = jnp.full((nmap.shape[0] - koff, rows), table, jnp.int32)
    owner_row = owners[...]
    owner_col = jnp.transpose(jnp.broadcast_to(owner_row, (8, rows)))[:, 0:1]
    row_at = lax.broadcasted_iota(jnp.int32, (rows, rows), 0)
    col_at = lax.broadcasted_iota(jnp.int32, (rows, rows), 1)
    earlier = jnp.where((owner_row == owner_col) & (row_at < col_at), 1, 0)
    tgt[...] = owner_row * recv.shape[1] + jnp.sum(earlier, axis=0, keepdims=True)
    masked, rscale, normed, pre = norm_parts(feat[...], active[...], gains)
    act = (pre / (1.0 + jnp.exp(-pre))).astype(BF16)
    lookup[0:rows, :] = act
    h = h_ref[0]
    share = act[0:BLK]
    for b in range(1, NB):
        share = jnp.where(h == b, act[b * BLK : (b + 1) * BLK].astype(F32), share.astype(F32)).astype(BF16)
    shared[...] = share
    for n, (ds, df) in enumerate(around):
        if ds == 0 and df == 0:
            lookup[rows + n * BLK : rows + (n + 1) * BLK, :] = share
        else:

            @pl.when(jnp.logical_not(inside(ds, df)))
            def _():
                lookup[rows + n * BLK : rows + (n + 1) * BLK, :] = jnp.zeros((BLK, C), BF16)

            @pl.when(jnp.logical_not(inside(-ds, -df)))
            def _():
                grecv[n] = jnp.zeros((BLK, C), BF16)

    rg = (og[...].astype(F32) * active[...])
    rgp[...] = regroup(
        rg, lambda p, r: p * width + r, lambda p, r: p * LANES + r, width, F
    ).astype(BF16)
    conv[...] = jnp.zeros_like(conv)

    barrier = pltpu.get_barrier_semaphore()
    for d in range(1, S):
        pl.semaphore_signal(barrier, inc=1, device_id=((s + d) % S, f), device_id_type=MESH)
    for d in range(1, F):
        pl.semaphore_signal(barrier, inc=1, device_id=(s, (f + d) % F), device_id_type=MESH)
    for ds, df in around:
        if ds and df:
            pl.semaphore_signal(
                barrier, inc=1, device_id=((s + ds + S) % S, (f + df + F) % F), device_id_type=MESH
            )
    pl.semaphore_wait(barrier, S + F - 2 + 4)

    def halo(n, ds, df):
        return remote(
            shared, lookup.at[pl.ds(rows + n * BLK, BLK)], hsend.at[n], hrecv.at[n], s - ds, f - df
        )

    def first(g, d):
        return remote(
            wire.at[g], wbuf.at[g, f, :, z, y], wsend.at[g, d - 1], wrecv.at[g, d - 1],
            ((z + d) % Z) * Y + y, f,
        )

    def passed(ref, g, i, ss, ff):
        return remote(ref, ref, wsend.at[g, i], wrecv.at[g, i], ss, ff)

    B0 = Z - 1
    low, high = pl.ds(0, Z // 2), pl.ds(Z // 2, Z - Z // 2)

    def second(g):
        return [
            passed(wbuf.at[g, f, :, low, y], g, B0, sy, f),
            passed(wbuf.at[g, f, :, high, y], g, B0 + 1, s, fx),
        ]

    def third(g):
        return [
            passed(wbuf.at[g, f, :, low], g, B0 + 2, s, fx),
            passed(wbuf.at[g, f, :, high, y], g, B0 + 3, sy, f),
            passed(wbuf.at[g, fx, :, high, y], g, B0 + 4, sy, f),
        ]

    def fourth(g):
        return [
            passed(wbuf.at[g, f], g, B0 + 5, s, fp),
            passed(wbuf.at[g, fx], g, B0 + 6, s, fp),
        ]

    for d in range(1, Z):
        first(0, d).start()
    for n, (ds, df) in enumerate(around):
        if ds or df:

            @pl.when(inside(-ds, -df))
            def _():
                halo(n, ds, df).start()

    @pl.loop(1, G)
    def _(g):
        for d in range(1, Z):
            first(g, d).start()

    own.wait()

    lane_u = lax.broadcasted_iota(jnp.int32, (rows, table), 1)

    def gather(k):
        line = jnp.broadcast_to(nmap[pl.ds(k, 1)], (8, rows))
        ids = jnp.transpose(line)[:, 0:1]
        pick = jnp.where(lane_u == ids, 1.0, 0.0).astype(BF16)
        pb[k] = jnp.dot(pick, lookup[...], preferred_element_type=F32).astype(BF16)

    def whole(g, j):
        return jnp.concatenate([wbuf[g, p, j].reshape(C, LANES) for p in range(F)], axis=1)

    def use(g, j, weights):
        k = g * K4 + j
        conv[...] += jnp.dot(pb[k], weights, preferred_element_type=F32)
        pb[k] = lax.dot_general(
            rgp[...], weights, (((1,), (1,)), ((), ())), preferred_element_type=F32
        ).astype(BF16)

    @pl.loop(0, G + 3)
    def _(t):
        @pl.when(t < G)
        def _():
            for d in range(1, Z):
                first(t, d).wait_recv()

            for c in second(t):
                c.start()

        @pl.when((t >= 1) & (t < G + 1))
        def _():
            for c in second(t - 1):
                c.wait_recv()
            for c in third(t - 1):
                c.start()

        @pl.when((t >= 2) & (t < G + 2))
        def _():
            for c in third(t - 2):
                c.wait_recv()
            for c in fourth(t - 2):
                c.start()

        @pl.when(t == 1)
        def _():
            for n, (ds, df) in enumerate(around):
                if ds or df:

                    @pl.when(inside(ds, df))
                    def _():
                        halo(n, ds, df).wait_recv()

        @pl.when((t >= 1) & (t < G + 1))
        def _():
            @pl.loop(0, K4)
            def _(j):
                gather((t - 1) * K4 + j)

        g5 = t - 3

        @pl.when(g5 >= 0)
        def _():
            for c in fourth(g5):
                c.wait_recv()
            lanes = lax.broadcasted_iota(jnp.int32, (C, LANES), 1)
            piece = LANES - width
            for p in range(F):
                tile = jnp.zeros((C, LANES), F32)
                for q in range(Q):
                    part = moved(wbuf[g5, p, q].reshape(C, LANES).astype(F32), q * piece - width)
                    tile = jnp.where((lanes >= q * piece) & (lanes < (q + 1) * piece), part, tile)
                w3[:, p * LANES : (p + 1) * LANES] = tile.astype(BF16)

            @pl.loop(0, Q)
            def _(j):
                use(g5, j, whole(g5, j))

            use(g5, Q, w3[...])

    total = regroup(conv[...], lambda p, r: p * LANES + r, lambda p, r: p * width + r, width, F)
    out = ((feat[...].astype(F32) * active[...] + total) * active[...]).astype(BF16)
    sec[...] = out
    cap = recv.shape[1]
    slots = lax.broadcasted_iota(jnp.int32, (S * cap, rows), 0)
    place = jnp.where(slots == tgt[...], 1.0, 0.0).astype(BF16)
    outbox[...] = jnp.dot(place, out, preferred_element_type=F32).astype(BF16).reshape(S, cap, C)

    def skip(d):
        o = (s + d) % S
        return remote(outbox.at[o], recv.at[s], ssend.at[d - 1], srecv.at[d - 1], o, f)

    def scatter(u0):
        def step(g, acc):
            base = lax.broadcasted_iota(jnp.int32, (rows, rows), 0) + u0
            hot = jnp.concatenate(
                [jnp.where(base == nmap[pl.ds(g * K4 + j, 1)], 1.0, 0.0).astype(BF16) for j in range(K4)], axis=1
            )
            return acc + jnp.dot(
                hot, pb[pl.ds(g * K4, K4)].reshape(K4 * rows, C), preferred_element_type=F32
            )

        return step

    def grad(n, ds, df):
        return remote(gsend.at[n], grecv.at[n], bsend.at[n], brecv.at[n], s + ds, f + df)

    per = rows // BLK

    def send_grads(c):
        for n in range(c * per, (c + 1) * per):
            ds, df = around[n]
            if ds or df:

                @pl.when(inside(ds, df))
                def _():
                    grad(n, ds, df).start()

    keep = pltpu.make_async_copy(outbox.at[s], recv.at[s], own_sem)

    @pl.loop(0, len(around) // per)
    def _(c):
        conv[:, 0:C] = jnp.zeros((rows, C), F32)

        @pl.loop(0, G)
        def _(g):
            conv[:, 0:C] = scatter((c + 1) * rows)(g, conv[:, 0:C])

        gsend[pl.ds(c * per, per)] = conv[:, 0:C].astype(BF16).reshape(per, BLK, C)

        @pl.when(c == 0)
        def _():
            for d in range(1, S):
                skip(d).start()
            keep.start()

        for cc in range(1, len(around) // per):

            @pl.when(c == cc)
            def _():
                send_grads(cc - 1)

        @pl.when(c == (len(around) // per) // 2)
        def _():
            lo = (len(around) // 2 % per) * BLK
            grecv[len(around) // 2] = conv[lo : lo + BLK, 0:C].astype(BF16)

    conv[:, 0:C] = scatter(0)(0, jnp.zeros((rows, C), F32))
    send_grads(len(around) // per - 1)

    @pl.loop(1, G)
    def _(g):
        conv[:, 0:C] = scatter(0)(g, conv[:, 0:C])

    for n, (ds, df) in enumerate(around):
        if ds or df:

            @pl.when(inside(-ds, -df))
            def _():
                grad(n, ds, df).wait_recv()

    back = jnp.zeros((BLK, C), F32)
    for n in range(len(around)):
        back = back + grecv[n].astype(F32)
    for b in range(NB):
        r0 = b * BLK
        act_b = active[r0 : r0 + BLK]
        masked, rscale, normed, pre = norm_parts(feat[r0 : r0 + BLK], act_b, gains)
        ag = conv[r0 : r0 + BLK, 0:C] + jnp.where(h == b, back, 0.0)
        sig = 1.0 / (1.0 + jnp.exp(-pre))
        ng = ag * sig * (1.0 + pre * (1.0 - sig)) * gains
        mg = rscale * (ng - normed * jnp.mean(ng * normed, axis=-1, keepdims=True))
        fgrad[r0 : r0 + BLK] = (
            (og[r0 : r0 + BLK].astype(F32) * act_b + mg) * act_b
        ).astype(BF16)

    keep.wait()
    for d in range(1, S):
        skip(d).wait()
    for n, (ds, df) in enumerate(around):
        if ds or df:

            @pl.when(inside(-ds, -df))
            def _():
                halo(n, ds, df).wait_send()

            @pl.when(inside(ds, df))
            def _():
                grad(n, ds, df).wait_send()

    @pl.loop(0, G)
    def _(g):
        for d in range(1, Z):
            first(g, d).wait_send()

        for c in second(g) + third(g) + fourth(g):
            c.wait_send()


def shards(mesh, features, channel_gain, conv_weight, kernel_map, counts, halo_list, skip_dest, out_grad):
    S, F = mesh.shape["space"], mesh.shape["fsdp"]
    koff, cin, width = conv_weight.shape
    rows, C = features.shape[2:]
    piece = LANES - width
    fits = F == 4 and S % 2 == 0 and cin % 16 == 0 and width == Q * piece and halo_list.shape[2] == 1
    if not (fits and rows == NB * BLK and 9 % NB == 0 and C == F * width):
        return shards_plain(
            features, channel_gain, conv_weight, kernel_map, counts, halo_list, skip_dest, out_grad
        )
    Z, K4 = S // 2, Q + 1
    G = -(-koff // K4)
    w = jnp.pad(conv_weight, ((0, G * K4 - koff), (0, 0), (0, 0))).reshape(G, K4, cin, width)
    extra = w[:, Q].reshape(G, cin, Q, piece).transpose(0, 2, 1, 3)
    wire = jnp.concatenate([w[:, :Q], extra], axis=-1)
    table = rows + 9 * BLK
    cap = max(2, 2 * rows // S)
    owners = skip_dest[0, 0].reshape(1, rows)
    vm = pl.BlockSpec(memory_space=pltpu.VMEM)
    dma = pltpu.SemaphoreType.DMA
    sec, fgrad, recv = pl.pallas_call(
        functools.partial(section_kernel, (S, F, Z, G, K4)),
        out_shape=(
            jax.ShapeDtypeStruct((rows, C), BF16),
            jax.ShapeDtypeStruct((rows, C), BF16),
            jax.ShapeDtypeStruct((S, cap, C), BF16),
        ),
        in_specs=[pl.BlockSpec(memory_space=pltpu.SMEM)] * 2 + [vm] * 6,
        out_specs=(vm, vm, vm),
        scratch_shapes=[
            pltpu.VMEM((rows, 1), F32),
            pltpu.VMEM((G * K4, rows), jnp.int32),
            pltpu.VMEM((1, rows), jnp.int32),
            pltpu.VMEM((G, F, Q, Z, 2, cin, LANES), BF16),
            pltpu.VMEM((table, C), BF16),
            pltpu.VMEM((G * K4, rows, C), BF16),
            pltpu.VMEM((rows, F * LANES), F32),
            pltpu.VMEM((BLK, C), BF16),
            pltpu.VMEM((rows, F * LANES), BF16),
            pltpu.VMEM((C, F * LANES), BF16),
            pltpu.VMEM((9, BLK, C), BF16),
            pltpu.VMEM((9, BLK, C), BF16),
            pltpu.VMEM((S, cap, C), BF16),
            dma((G, Z + 6)),
            dma((G, Z + 6)),
            dma((9,)),
            dma((9,)),
            dma((S - 1,)),
            dma((S - 1,)),
            dma((9,)),
            dma((9,)),
            dma,
        ],
        compiler_params=pltpu.CompilerParams(collective_id=0, has_side_effects=True),
        name="section",
    )(
        halo_list[0, 0], counts[0, 0], features[0, 0], channel_gain, out_grad[0, 0], wire, kernel_map[0, 0], owners
    )
    return (sec[None, None], fgrad[None, None], recv[None, None])


def solution(mesh):
    return jax.shard_map(
        functools.partial(shards, mesh),
        mesh=mesh,
        in_specs=(
            P("space", "fsdp", None, None),
            P(),
            P(None, "space", "fsdp"),
            P("space", "fsdp", None, None),
            P("space", "fsdp", None),
            P("space", "fsdp", None),
            P("space", "fsdp", None, None),
            P("space", "fsdp", None, None),
        ),
        out_specs=(
            P("space", "fsdp", None, None),
            P("space", "fsdp", None, None),
            P("space", "fsdp", None, None, None),
        ),
        check_vma=False,
    )
```

```python
import functools

import jax
import jax.numpy as jnp
from jax import lax
from jax.experimental import pallas as pl
from jax.experimental.pallas import tpu as pltpu
from jax.sharding import PartitionSpec as P

BLK = 128
KOFF = 27
HB = 1
NB = 3
ROWS = 1536


NORM_EPS = 1e-06


def padded(cells, sides, width):
    for axis, dim in sides:
        count = lax.axis_size(axis)
        ends = count - 1
        head = lax.slice_in_dim(cells, 0, width, axis=dim)
        tail = lax.slice_in_dim(cells, cells.shape[dim] - width, cells.shape[dim], axis=dim)
        cells = jnp.concatenate(
            [
                lax.ppermute(tail, axis, [(i, (i + 1) % count) for i in range(ends)]),
                cells,
                lax.ppermute(head, axis, [((i + 1) % count, i) for i in range(ends)]),
            ],
            axis=dim,
        )
    return cells


def passed_along(x, axis, by):
    count = lax.axis_size(axis)
    pairs = [(i, i + by) for i in range(count) if 0 <= i + by < count]
    return lax.ppermute(x, axis, pairs)


def shards_plain(features, channel_gain, conv_weight, kernel_map, counts, halo_list, skip_dest, out_grad):
    own_rows = features[0, 0]
    rowcount = own_rows.shape[0]
    width = own_rows.shape[1]
    slot_ids = jnp.arange(rowcount, dtype=jnp.int32)
    limits = jnp.repeat(counts[0, 0], BLK)
    active = (slot_ids % BLK < limits).astype(jnp.float32)[:, None]
    masked = own_rows * active.astype(jnp.bfloat16)
    masked_f = masked.astype(jnp.float32)
    rscale = lax.rsqrt(jnp.mean(masked_f * masked_f, axis=-1, keepdims=True) + NORM_EPS)
    normed = masked_f * rscale
    pre_act = normed * channel_gain
    act = jax.nn.silu(pre_act).astype(jnp.bfloat16)
    shared = act.reshape(NB, BLK, width)[halo_list[0, 0]]
    beside_all = padded(shared[None, None], (("space", 0), ("fsdp", 1)), 1)
    lookup = jnp.concatenate(
        [act, beside_all.reshape(9 * HB * BLK, width), jnp.zeros((1, width), jnp.bfloat16)], axis=0
    )
    row_grad = out_grad[0, 0] * active.astype(jnp.bfloat16)
    groups = KOFF // 3
    weight_groups = conv_weight.reshape(groups, 3, conv_weight.shape[1], conv_weight.shape[2])
    map_groups = kernel_map[0, 0].reshape(groups, 3, rowcount)

    def group_step(state, inputs_g):
        running, table_grad = state
        weight_piece, neighbours = inputs_g
        widened = lax.all_gather(weight_piece, "fsdp", axis=2, tiled=True)
        full_weights = lax.all_gather(widened, "space", axis=1, tiled=True)
        picked = lookup[neighbours]
        running = running + jnp.einsum(
            "kvc,kcd->vd", picked, full_weights, preferred_element_type=jnp.float32
        )
        backward = jnp.einsum(
            "vd,kcd->kvc", row_grad, full_weights, preferred_element_type=jnp.float32
        )
        table_grad = table_grad.at[neighbours.reshape(-1)].add(backward.reshape(-1, width))
        return ((running, table_grad), None)

    start = (jnp.zeros((rowcount, width), jnp.float32), jnp.zeros((ROWS + 1, width), jnp.float32))
    (conv_sum, table_grad), _ = lax.scan(group_step, start, (weight_groups, map_groups))
    section_out = ((masked_f + conv_sum) * active).astype(jnp.bfloat16)
    owners = skip_dest[0, 0, :, 0]
    earlier = (owners[None, :] == owners[:, None]) & (slot_ids[None, :] < slot_ids[:, None])
    placing = jnp.sum(earlier.astype(jnp.int32), axis=1)
    space_size = lax.axis_size("space")
    capacity = max(2, 2 * rowcount // space_size)
    outbox = (
        jnp.zeros((space_size * capacity, width), jnp.bfloat16)
        .at[owners * capacity + placing]
        .set(section_out)
    )
    received = lax.all_to_all(
        outbox.reshape(space_size, capacity, width),
        "space",
        split_axis=0,
        concat_axis=0,
        tiled=True,
    )
    halo_grad = table_grad[rowcount : rowcount + 9 * HB * BLK].reshape(3, 3, HB, BLK, width)
    middle = halo_grad[1]
    for direction in (1, -1):
        middle = middle + passed_along(
            halo_grad[1 + direction].astype(jnp.bfloat16), "space", direction
        ).astype(jnp.float32)
    returned = middle[1]
    for direction in (1, -1):
        returned = returned + passed_along(
            middle[1 + direction].astype(jnp.bfloat16), "fsdp", direction
        ).astype(jnp.float32)
    act_grad = table_grad[:rowcount].reshape(NB, BLK, width).at[halo_list[0, 0]].add(returned)
    act_grad = act_grad.reshape(rowcount, width)
    sigmoid_pre = jax.nn.sigmoid(pre_act)
    pre_grad = act_grad * sigmoid_pre * (1.0 + pre_act * (1.0 - sigmoid_pre))
    normed_grad = pre_grad * channel_gain
    masked_grad = rscale * (
        normed_grad - normed * jnp.mean(normed_grad * normed, axis=-1, keepdims=True)
    )
    feature_grad = ((row_grad.astype(jnp.float32) + masked_grad) * active).astype(jnp.bfloat16)
    return (section_out[None, None], feature_grad[None, None], received[None, None])


LANES = 128
Q = 3
MESH = pl.DeviceIdType.MESH
F32 = jnp.float32
BF16 = jnp.bfloat16


def moved(x, shift):
    shift = shift % LANES
    return x if shift == 0 else pltpu.roll(x, shift, 1)


def regroup(x, from_of, to_of, width, pieces):
    lanes = lax.broadcasted_iota(jnp.int32, (x.shape[0], LANES), 1)
    tiles = {}
    for p in range(pieces):
        r = 0
        while r < width:
            src, dst = from_of(p, r), to_of(p, r)
            span = min(width - r, LANES - src % LANES, LANES - dst % LANES)
            at = src // LANES * LANES
            value = moved(x[:, at : at + LANES], dst - src)
            low = dst % LANES
            held = tiles.get(dst // LANES, jnp.zeros_like(value))
            tiles[dst // LANES] = jnp.where((lanes >= low) & (lanes < low + span), value, held)
            r += span
    return jnp.concatenate([tiles[t] for t in range(len(tiles))], axis=1)


def norm_parts(feat, active, gain):
    masked = feat.astype(F32) * active
    rscale = lax.rsqrt(jnp.mean(masked * masked, axis=-1, keepdims=True) + NORM_EPS)
    normed = masked * rscale
    return masked, rscale, normed, normed * gain


def section_kernel(
    dims, h_ref, counts, feat, gain, og, wire, maps, owners,
    sec, fgrad, recv,
    active, nmap, tgt, wbuf, lookup, pb, conv, shared, rgp, w3, gsend, grecv, outbox,
    wsend, wrecv, hsend, hrecv, ssend, srecv, bsend, brecv, own_sem,
):
    S, F, Z, G, K4 = dims
    Y = 2
    rows, C = feat.shape
    width = C // F
    table = lookup.shape[0]
    s = lax.axis_index("space")
    f = lax.axis_index("fsdp")
    z, y = s // Y, s % Y
    fx = (f + 2) % F
    fp = f + 1 - 2 * (f % 2)
    sy = s + 1 - 2 * y

    def remote(src, dst, a, b, ss, ff):
        return pltpu.make_async_remote_copy(
            src_ref=src, dst_ref=dst, send_sem=a, recv_sem=b, device_id=(ss, ff), device_id_type=MESH
        )

    def inside(ds, df):
        return (s + ds >= 0) & (s + ds < S) & (f + df >= 0) & (f + df < F)

    around = [(ds, df) for ds in (-1, 0, 1) for df in (-1, 0, 1)]

    own = pltpu.make_async_copy(wire, wbuf.at[:, f, :, z, y], own_sem)
    own.start()
    slot = lax.broadcasted_iota(jnp.int32, (BLK, 1), 0)
    for b in range(NB):
        active[b * BLK : (b + 1) * BLK] = jnp.where(slot < counts[b], 1.0, 0.0)
    gains = gain[...].reshape(1, C)
    koff = maps.shape[0]
    nmap[0:koff] = maps[...]
    nmap[koff:] = jnp.full((nmap.shape[0] - koff, rows), table, jnp.int32)
    owner_row = owners[...]
    owner_col = jnp.transpose(jnp.broadcast_to(owner_row, (8, rows)))[:, 0:1]
    row_at = lax.broadcasted_iota(jnp.int32, (rows, rows), 0)
    col_at = lax.broadcasted_iota(jnp.int32, (rows, rows), 1)
    earlier = jnp.where((owner_row == owner_col) & (row_at < col_at), 1, 0)
    tgt[...] = owner_row * recv.shape[1] + jnp.sum(earlier, axis=0, keepdims=True)
    masked, rscale, normed, pre = norm_parts(feat[...], active[...], gains)
    act = (pre / (1.0 + jnp.exp(-pre))).astype(BF16)
    lookup[0:rows, :] = act
    h = h_ref[0]
    share = act[0:BLK]
    for b in range(1, NB):
        share = jnp.where(h == b, act[b * BLK : (b + 1) * BLK].astype(F32), share.astype(F32)).astype(BF16)
    shared[...] = share
    for n, (ds, df) in enumerate(around):
        if ds == 0 and df == 0:
            lookup[rows + n * BLK : rows + (n + 1) * BLK, :] = share
        else:

            @pl.when(jnp.logical_not(inside(ds, df)))
            def _():
                lookup[rows + n * BLK : rows + (n + 1) * BLK, :] = jnp.zeros((BLK, C), BF16)

            @pl.when(jnp.logical_not(inside(-ds, -df)))
            def _():
                grecv[n] = jnp.zeros((BLK, C), BF16)

    rg = (og[...].astype(F32) * active[...])
    rgp[...] = regroup(
        rg, lambda p, r: p * width + r, lambda p, r: p * LANES + r, width, F
    ).astype(BF16)
    conv[...] = jnp.zeros_like(conv)

    barrier = pltpu.get_barrier_semaphore()
    for d in range(1, S):
        pl.semaphore_signal(barrier, inc=1, device_id=((s + d) % S, f), device_id_type=MESH)
    for d in range(1, F):
        pl.semaphore_signal(barrier, inc=1, device_id=(s, (f + d) % F), device_id_type=MESH)
    for ds, df in around:
        if ds and df:
            pl.semaphore_signal(
                barrier, inc=1, device_id=((s + ds + S) % S, (f + df + F) % F), device_id_type=MESH
            )
    pl.semaphore_wait(barrier, S + F - 2 + 4)

    def halo(n, ds, df):
        return remote(
            shared, lookup.at[pl.ds(rows + n * BLK, BLK)], hsend.at[n], hrecv.at[n], s - ds, f - df
        )

    def first(g, d):
        return remote(
            wire.at[g], wbuf.at[g, f, :, z, y], wsend.at[g, d - 1], wrecv.at[g, d - 1],
            ((z + d) % Z) * Y + y, f,
        )

    def passed(ref, g, i, ss, ff):
        return remote(ref, ref, wsend.at[g, i], wrecv.at[g, i], ss, ff)

    B0 = Z - 1
    low, high = pl.ds(0, Z // 2), pl.ds(Z // 2, Z - Z // 2)

    def second(g):
        return [
            passed(wbuf.at[g, f, :, low, y], g, B0, sy, f),
            passed(wbuf.at[g, f, :, high, y], g, B0 + 1, s, fx),
        ]

    def third(g):
        return [
            passed(wbuf.at[g, f, :, low], g, B0 + 2, s, fx),
            passed(wbuf.at[g, f, :, high, y], g, B0 + 3, sy, f),
            passed(wbuf.at[g, fx, :, high, y], g, B0 + 4, sy, f),
        ]

    def fourth(g):
        return [
            passed(wbuf.at[g, f], g, B0 + 5, s, fp),
            passed(wbuf.at[g, fx], g, B0 + 6, s, fp),
        ]

    for d in range(1, Z):
        first(0, d).start()
    for n, (ds, df) in enumerate(around):
        if ds or df:

            @pl.when(inside(-ds, -df))
            def _():
                halo(n, ds, df).start()

    @pl.loop(1, G)
    def _(g):
        for d in range(1, Z):
            first(g, d).start()

    own.wait()

    lane_u = lax.broadcasted_iota(jnp.int32, (rows, table), 1)

    def gather(k):
        line = jnp.broadcast_to(nmap[pl.ds(k, 1)], (8, rows))
        ids = jnp.transpose(line)[:, 0:1]
        pick = jnp.where(lane_u == ids, 1.0, 0.0).astype(BF16)
        pb[k] = jnp.dot(pick, lookup[...], preferred_element_type=F32).astype(BF16)

    def whole(g, j):
        return jnp.concatenate([wbuf[g, p, j].reshape(C, LANES) for p in range(F)], axis=1)

    def use(g, j, weights):
        k = g * K4 + j
        conv[...] += jnp.dot(pb[k], weights, preferred_element_type=F32)
        pb[k] = lax.dot_general(
            rgp[...], weights, (((1,), (1,)), ((), ())), preferred_element_type=F32
        ).astype(BF16)

    @pl.loop(0, G + 3)
    def _(t):
        @pl.when(t < G)
        def _():
            for d in range(1, Z):
                first(t, d).wait_recv()

            for c in second(t):
                c.start()

        @pl.when((t >= 1) & (t < G + 1))
        def _():
            for c in second(t - 1):
                c.wait_recv()
            for c in third(t - 1):
                c.start()

        @pl.when((t >= 2) & (t < G + 2))
        def _():
            for c in third(t - 2):
                c.wait_recv()
            for c in fourth(t - 2):
                c.start()

        @pl.when(t == 1)
        def _():
            for n, (ds, df) in enumerate(around):
                if ds or df:

                    @pl.when(inside(ds, df))
                    def _():
                        halo(n, ds, df).wait_recv()

        @pl.when((t >= 1) & (t < G + 1))
        def _():
            @pl.loop(0, K4)
            def _(j):
                gather((t - 1) * K4 + j)

        g5 = t - 3

        @pl.when(g5 >= 0)
        def _():
            for c in fourth(g5):
                c.wait_recv()
            lanes = lax.broadcasted_iota(jnp.int32, (C, LANES), 1)
            piece = LANES - width
            for p in range(F):
                tile = jnp.zeros((C, LANES), F32)
                for q in range(Q):
                    part = moved(wbuf[g5, p, q].reshape(C, LANES).astype(F32), q * piece - width)
                    tile = jnp.where((lanes >= q * piece) & (lanes < (q + 1) * piece), part, tile)
                w3[:, p * LANES : (p + 1) * LANES] = tile.astype(BF16)

            @pl.loop(0, Q)
            def _(j):
                use(g5, j, whole(g5, j))

            use(g5, Q, w3[...])

    total = regroup(conv[...], lambda p, r: p * LANES + r, lambda p, r: p * width + r, width, F)
    out = ((feat[...].astype(F32) * active[...] + total) * active[...]).astype(BF16)
    sec[...] = out
    cap = recv.shape[1]
    slots = lax.broadcasted_iota(jnp.int32, (S * cap, rows), 0)
    place = jnp.where(slots == tgt[...], 1.0, 0.0).astype(BF16)
    outbox[...] = jnp.dot(place, out, preferred_element_type=F32).astype(BF16).reshape(S, cap, C)

    def skip(d):
        o = (s + d) % S
        return remote(outbox.at[o], recv.at[s], ssend.at[d - 1], srecv.at[d - 1], o, f)

    def scatter(u0):
        def step(g, acc):
            base = lax.broadcasted_iota(jnp.int32, (rows, rows), 0) + u0
            hot = jnp.concatenate(
                [jnp.where(base == nmap[pl.ds(g * K4 + j, 1)], 1.0, 0.0).astype(BF16) for j in range(K4)], axis=1
            )
            return acc + jnp.dot(
                hot, pb[pl.ds(g * K4, K4)].reshape(K4 * rows, C), preferred_element_type=F32
            )

        return step

    def grad(n, ds, df):
        return remote(gsend.at[n], grecv.at[n], bsend.at[n], brecv.at[n], s + ds, f + df)

    per = rows // BLK

    def send_grads(c):
        for n in range(c * per, (c + 1) * per):
            ds, df = around[n]
            if ds or df:

                @pl.when(inside(ds, df))
                def _():
                    grad(n, ds, df).start()

    keep = pltpu.make_async_copy(outbox.at[s], recv.at[s], own_sem)

    @pl.loop(0, len(around) // per)
    def _(c):
        conv[:, 0:C] = jnp.zeros((rows, C), F32)

        @pl.loop(0, G)
        def _(g):
            conv[:, 0:C] = scatter((c + 1) * rows)(g, conv[:, 0:C])

            @pl.when((c == 0) & (g == 0))
            def _():
                for d in range(1, S):
                    skip(d).start()
                keep.start()

        gsend[pl.ds(c * per, per)] = conv[:, 0:C].astype(BF16).reshape(per, BLK, C)

        for cc in range(1, len(around) // per):

            @pl.when(c == cc)
            def _():
                send_grads(cc - 1)

        @pl.when(c == (len(around) // per) // 2)
        def _():
            lo = (len(around) // 2 % per) * BLK
            grecv[len(around) // 2] = conv[lo : lo + BLK, 0:C].astype(BF16)

    conv[:, 0:C] = scatter(0)(0, jnp.zeros((rows, C), F32))
    send_grads(len(around) // per - 1)

    @pl.loop(1, G)
    def _(g):
        conv[:, 0:C] = scatter(0)(g, conv[:, 0:C])

    for n, (ds, df) in enumerate(around):
        if ds or df:

            @pl.when(inside(-ds, -df))
            def _():
                grad(n, ds, df).wait_recv()

    back = jnp.zeros((BLK, C), F32)
    for n in range(len(around)):
        back = back + grecv[n].astype(F32)
    for b in range(NB):
        r0 = b * BLK
        act_b = active[r0 : r0 + BLK]
        masked, rscale, normed, pre = norm_parts(feat[r0 : r0 + BLK], act_b, gains)
        ag = conv[r0 : r0 + BLK, 0:C] + jnp.where(h == b, back, 0.0)
        sig = 1.0 / (1.0 + jnp.exp(-pre))
        ng = ag * sig * (1.0 + pre * (1.0 - sig)) * gains
        mg = rscale * (ng - normed * jnp.mean(ng * normed, axis=-1, keepdims=True))
        fgrad[r0 : r0 + BLK] = (
            (og[r0 : r0 + BLK].astype(F32) * act_b + mg) * act_b
        ).astype(BF16)

    keep.wait()
    for d in range(1, S):
        skip(d).wait()
    for n, (ds, df) in enumerate(around):
        if ds or df:

            @pl.when(inside(-ds, -df))
            def _():
                halo(n, ds, df).wait_send()

            @pl.when(inside(ds, df))
            def _():
                grad(n, ds, df).wait_send()

    @pl.loop(0, G)
    def _(g):
        for d in range(1, Z):
            first(g, d).wait_send()

        for c in second(g) + third(g) + fourth(g):
            c.wait_send()


def shards(mesh, features, channel_gain, conv_weight, kernel_map, counts, halo_list, skip_dest, out_grad):
    S, F = mesh.shape["space"], mesh.shape["fsdp"]
    koff, cin, width = conv_weight.shape
    rows, C = features.shape[2:]
    piece = LANES - width
    fits = F == 4 and S % 2 == 0 and cin % 16 == 0 and width == Q * piece and halo_list.shape[2] == 1
    if not (fits and rows == NB * BLK and 9 % NB == 0 and C == F * width):
        return shards_plain(
            features, channel_gain, conv_weight, kernel_map, counts, halo_list, skip_dest, out_grad
        )
    Z, K4 = S // 2, Q + 1
    G = -(-koff // K4)
    w = jnp.pad(conv_weight, ((0, G * K4 - koff), (0, 0), (0, 0))).reshape(G, K4, cin, width)
    extra = w[:, Q].reshape(G, cin, Q, piece).transpose(0, 2, 1, 3)
    wire = jnp.concatenate([w[:, :Q], extra], axis=-1)
    table = rows + 9 * BLK
    cap = max(2, 2 * rows // S)
    owners = skip_dest[0, 0].reshape(1, rows)
    vm = pl.BlockSpec(memory_space=pltpu.VMEM)
    dma = pltpu.SemaphoreType.DMA
    sec, fgrad, recv = pl.pallas_call(
        functools.partial(section_kernel, (S, F, Z, G, K4)),
        out_shape=(
            jax.ShapeDtypeStruct((rows, C), BF16),
            jax.ShapeDtypeStruct((rows, C), BF16),
            jax.ShapeDtypeStruct((S, cap, C), BF16),
        ),
        in_specs=[pl.BlockSpec(memory_space=pltpu.SMEM)] * 2 + [vm] * 6,
        out_specs=(vm, vm, vm),
        scratch_shapes=[
            pltpu.VMEM((rows, 1), F32),
            pltpu.VMEM((G * K4, rows), jnp.int32),
            pltpu.VMEM((1, rows), jnp.int32),
            pltpu.VMEM((G, F, Q, Z, 2, cin, LANES), BF16),
            pltpu.VMEM((table, C), BF16),
            pltpu.VMEM((G * K4, rows, C), BF16),
            pltpu.VMEM((rows, F * LANES), F32),
            pltpu.VMEM((BLK, C), BF16),
            pltpu.VMEM((rows, F * LANES), BF16),
            pltpu.VMEM((C, F * LANES), BF16),
            pltpu.VMEM((9, BLK, C), BF16),
            pltpu.VMEM((9, BLK, C), BF16),
            pltpu.VMEM((S, cap, C), BF16),
            dma((G, Z + 6)),
            dma((G, Z + 6)),
            dma((9,)),
            dma((9,)),
            dma((S - 1,)),
            dma((S - 1,)),
            dma((9,)),
            dma((9,)),
            dma,
        ],
        compiler_params=pltpu.CompilerParams(collective_id=0, has_side_effects=True),
        name="section",
    )(
        halo_list[0, 0], counts[0, 0], features[0, 0], channel_gain, out_grad[0, 0], wire, kernel_map[0, 0], owners
    )
    return (sec[None, None], fgrad[None, None], recv[None, None])


def solution(mesh):
    return jax.shard_map(
        functools.partial(shards, mesh),
        mesh=mesh,
        in_specs=(
            P("space", "fsdp", None, None),
            P(),
            P(None, "space", "fsdp"),
            P("space", "fsdp", None, None),
            P("space", "fsdp", None),
            P("space", "fsdp", None),
            P("space", "fsdp", None, None),
            P("space", "fsdp", None, None),
        ),
        out_specs=(
            P("space", "fsdp", None, None),
            P("space", "fsdp", None, None),
            P("space", "fsdp", None, None, None),
        ),
        check_vma=False,
    )
```
